32 devices in a mesh: segment: 4 (over z), seq: 8 (over y, x, core).
Axes of the slice: x: 2, y: 2, z: 4, core: 2. Of those that a mesh axis runs over, the one named last changes fastest.
Arguments:
- query: bfloat16 [4, 1024, 2048], P('segment', 'seq'), may hold values from -6 to 6
- key: bfloat16 [4, 1024, 2048], P('segment', 'seq'), may hold values from -6 to 6
- value: bfloat16 [4, 1024, 2048], P('segment', 'seq'), may hold values from -6 to 6
- cotangent: bfloat16 [4, 1024, 2048], P('segment', 'seq'), may hold values from -96 to 96
- block_order: int32 [4, 4, 4], P('segment'), may hold values from 0 to 3, each once within a row
Outputs:
- passed_rows: bfloat16 [4, 1024, 2048], P('segment', 'seq')
- grad_query: bfloat16 [4, 1024, 2048], P('segment', 'seq')
- grad_key: bfloat16 [4, 1024, 2048], P('segment', 'seq')
- grad_value: bfloat16 [4, 1024, 2048], P('segment', 'seq')
The draws below stay inside these ranges and needn't reach their ends.
Inputs may be any that keep to these rules, and one draw needn't show every extreme that they name: `block_order`: each row names every block of the section once.
All inputs are finite; a program needn't handle non-finite values.
Results may differ from the reference program's by a relative error of at most 0.0071.
Values may be sent and summed in bfloat16 or wider, within the bound.
A program may use at most 128 MiB of HBM per device.

```python
import math
import jax
import jax.numpy as jnp
from jax import lax

HEADS = 16
HEAD_DIM = 128
GROUPS = 4
BLOCK = 256
TOK_DEV = 128
BLOCKS = 4
SEQ_LEN = 1024
FEATURES = 2048
SEGMENTS = 4


def draw_pair(key, which):
    folded = jax.random.fold_in(key, which)
    query_seed, key_seed = jax.random.split(folded, 2)
    full_shape = (SEGMENTS, SEQ_LEN, FEATURES)
    queries = jnp.clip(jax.random.normal(query_seed, full_shape), -4.0, 4.0)
    key_draw = jnp.clip(jax.random.normal(key_seed, full_shape), -4.0, 4.0)
    return (queries, key_draw)


def draw_query(key, part):
    return draw_pair(key, 11)[0].astype(jnp.bfloat16)


def draw_key(key, part):
    return draw_pair(key, 11)[1].astype(jnp.bfloat16)


def steps_of(own_key, dims, cuts, smallest, largest):
    gain, own = 1.0, jax.random.fold_in(own_key, 6)
    for dim, parts in cuts:
        steps = jnp.exp(jax.random.uniform(jax.random.fold_in(own, dim), (parts,), jnp.float32, smallest / len(cuts), largest / len(cuts)))
        gain = gain * jnp.repeat(steps, dims[dim] // parts).reshape([-1 if axis == dim else 1 for axis in range(len(dims))])
    return gain


def centred(rng, extent, deviation, most, cuts=(), kind=jnp.bfloat16):
    gain = steps_of(rng, extent, cuts, -0.22, 0.18) if cuts else 1.0
    drawn = jax.random.normal(rng, extent, jnp.float32) * deviation * gain
    return jnp.minimum(jnp.maximum(drawn, -most), most).astype(kind)


def setup_inputs(seed: int = 0) -> dict:
    seeds = jax.random.split(jax.random.key(seed), 6)
    return {
        "query": draw_query(jax.random.fold_in(seeds[5], 71), 0),
        "key": draw_key(jax.random.fold_in(seeds[5], 71), 0),
        "value": centred(seeds[2], (SEGMENTS, SEQ_LEN, FEATURES), 1.0, 6.0, ((0, 4), (1, 8))),
        "cotangent": centred(seeds[3], (SEGMENTS, SEQ_LEN, FEATURES), 16.0, 96.0, ((0, 4), (1, 8))),
        "block_order": jax.vmap(lambda own: jax.random.permutation(own, BLOCKS))(jax.random.split(seeds[4], SEGMENTS * GROUPS)).reshape((SEGMENTS, GROUPS, BLOCKS)).astype(jnp.int32),
    }


def split_heads(block_rows):
    return block_rows.astype(jnp.float32).reshape(block_rows.shape[0], HEADS, HEAD_DIM)

def attention_probs(queries, key_rows):
    score_scale = 1.0 / math.sqrt(HEAD_DIM)
    scores = jnp.einsum('qhd,khd->hqk', split_heads(queries), split_heads(key_rows)) * score_scale
    top_score = lax.optimization_barrier(jnp.max(scores, axis=-1, keepdims=True))
    expo_terms = jnp.exp(scores - top_score)
    return expo_terms / lax.optimization_barrier(jnp.sum(expo_terms, axis=-1, keepdims=True))

def rounded_sum(first_term, second_term):
    total = lax.optimization_barrier((first_term + second_term).astype(jnp.bfloat16))
    return total.astype(jnp.float32)

def round_trip(values):
    return lax.optimization_barrier(values.astype(jnp.bfloat16)).astype(jnp.float32)

def block_pass(queries, key_rows, value_rows, out_grads):
    score_scale = 1.0 / math.sqrt(HEAD_DIM)
    probs = attention_probs(queries, key_rows)
    probs_low = round_trip(probs)
    value_heads = split_heads(value_rows)
    attended = jnp.einsum('hqk,khd->qhd', probs_low, value_heads)
    attended = attended.reshape(BLOCK, FEATURES).astype(jnp.bfloat16)
    grad_heads = split_heads(out_grads)
    query_heads = split_heads(queries)
    grad_probs = jnp.einsum('qhd,khd->hqk', grad_heads, value_heads)
    row_dot = lax.optimization_barrier(jnp.sum(probs * grad_probs, axis=-1, keepdims=True))
    grad_scores = round_trip(probs * (grad_probs - row_dot) * score_scale)
    grad_queries = jnp.einsum('hqk,khd->qhd', grad_scores, split_heads(key_rows))
    grad_queries = grad_queries.reshape(BLOCK, FEATURES).astype(jnp.bfloat16)
    key_count = key_rows.shape[0]
    halves_key = []
    halves_value = []
    for half_index in range(2):
        low = half_index * TOK_DEV
        high = low + TOK_DEV
        key_part = jnp.einsum('hqk,qhd->khd', grad_scores[:, low:high], query_heads[low:high])
        value_part = jnp.einsum('hqk,qhd->khd', probs_low[:, low:high], grad_heads[low:high])
        halves_key.append(round_trip(key_part.reshape(key_count, FEATURES)))
        halves_value.append(round_trip(value_part.reshape(key_count, FEATURES)))
    key_own = halves_key[0][:BLOCK] + halves_key[1][:BLOCK]
    value_own = halves_value[0][:BLOCK] + halves_value[1][:BLOCK]
    key_far = rounded_sum(halves_key[0][BLOCK:], halves_key[1][BLOCK:])
    value_far = rounded_sum(halves_value[0][BLOCK:], halves_value[1][BLOCK:])
    return (attended, grad_queries, key_own, key_far, value_own, value_far)

def matched_rows(blocks, order):
    grouped = blocks.reshape(BLOCKS, BLOCK, GROUPS, FEATURES // GROUPS)
    picked = [jnp.take(grouped[:, :, group_index, :], order[group_index], axis=0) for group_index in range(GROUPS)]
    return jnp.stack(picked, axis=2).reshape(BLOCKS, BLOCK, FEATURES)

def return_rows(own_terms, far_terms, order):
    grouped_own = own_terms.reshape(BLOCKS, BLOCK, GROUPS, FEATURES // GROUPS)
    grouped_far = far_terms.reshape(BLOCKS, BLOCK, GROUPS, FEATURES // GROUPS)
    columns = []
    for group_index in range(GROUPS):
        column = grouped_own[:, :, group_index, :].at[order[group_index]].add(grouped_far[:, :, group_index, :])
        columns.append(column)
    return jnp.stack(columns, axis=2).reshape(SEQ_LEN, FEATURES).astype(jnp.bfloat16)

def reference(query, key, value, cotangent, block_order):
    attended_all = []
    query_grads = []
    key_grads = []
    value_grads = []
    for segment_index in range(SEGMENTS):
        order = block_order[segment_index].astype(jnp.int32)
        queries = query[segment_index].reshape(BLOCKS, BLOCK, FEATURES)
        key_blocks = key[segment_index].reshape(BLOCKS, BLOCK, FEATURES)
        value_blocks = value[segment_index].reshape(BLOCKS, BLOCK, FEATURES)
        out_grads = cotangent[segment_index].reshape(BLOCKS, BLOCK, FEATURES)
        key_sets = jnp.concatenate([key_blocks, matched_rows(key_blocks, order)], axis=1)
        value_sets = jnp.concatenate([value_blocks, matched_rows(value_blocks, order)], axis=1)
        results = lax.map(lambda blocks_in: block_pass(*blocks_in), (queries, key_sets, value_sets, out_grads))
        attended_all.append(results[0].reshape(SEQ_LEN, FEATURES))
        query_grads.append(results[1].reshape(SEQ_LEN, FEATURES))
        key_grads.append(return_rows(results[2], results[3], order))
        value_grads.append(return_rows(results[4], results[5], order))
    passed_rows = jnp.roll(jnp.stack(attended_all), 1, axis=0)
    return (passed_rows, jnp.stack(query_grads), jnp.stack(key_grads), jnp.stack(value_grads))
```

```python
import functools
import math

import jax
import jax.numpy as jnp
from jax import lax
from jax.experimental import pallas as pl
from jax.experimental.pallas import tpu as pltpu
from jax.sharding import PartitionSpec as P

HEADS = 16
HEAD_DIM = 128
GROUPS = 4
BLOCK = 256
TOK_DEV = 128
FEATURES = 2048
ORDER = (2, 4, 6, 3, 5, 7, 1)


def from_partner_2(shard, axis, bit):
    return lax.ppermute(shard, axis, [(i, i ^ 1 << bit) for i in range(lax.axis_size(axis))])


def from_behind(value, axis, steps):
    count = lax.axis_size(axis)
    pairs = [(source, (source + steps) % count) for source in range(count)]
    return lax.ppermute(value, axis, pairs)


def partner_rows(stacked):
    return from_partner_2(stacked, "seq", 0)


def chosen(slots, wanted):
    mask = (wanted[:, None] == jnp.arange(slots.shape[1])[None, :]).astype(slots.dtype)
    return jnp.einsum(
        "ts,csrw->ctrw", mask, slots, preferred_element_type=jnp.float32
    ).astype(slots.dtype)


def routed(stacked, table, group_count):
    devices = lax.axis_size("seq")
    channels, slot_count, row_count, width = stacked.shape
    piece_rows = row_count // devices
    pieces = stacked.reshape(channels, slot_count, devices, piece_rows * width)
    arrived = lax.all_to_all(pieces, "seq", split_axis=2, concat_axis=2, tiled=True)
    arrived = arrived.reshape(
        channels, slot_count * devices, piece_rows, group_count, width // group_count
    )
    picked = [
        chosen(arrived[:, :, :, group_index, :], table[group_index])
        for group_index in range(group_count)
    ]
    fanout = table.shape[1] // devices
    outward = jnp.stack(picked, axis=3).reshape(channels, fanout, devices, piece_rows * width)
    landed = lax.all_to_all(outward, "seq", split_axis=2, concat_axis=2, tiled=True)
    return landed.reshape(channels, fanout, row_count, width)


def route_tables(order, devices):
    device_ids = jnp.arange(devices, dtype=jnp.int32)
    half_ids = jnp.arange(2, dtype=jnp.int32)
    group_count = order.shape[0]
    target = jnp.take(order, device_ids // 2, axis=1)
    both_halves = (2 * target[:, None, :] + half_ids[None, :, None]).reshape(
        group_count, 2 * devices
    )
    same_half = 2 * target + device_ids % 2
    inverse = jnp.argsort(order, axis=1)
    asking = 2 * jnp.take(inverse, device_ids // 2, axis=1)
    returning = (
        (device_ids % 2)[None, None, :] * devices + asking[:, None, :] + half_ids[None, :, None]
    ).reshape(group_count, 2 * devices)
    summed_back = asking + device_ids % 2
    return (both_halves, same_half, returning, summed_back)


def head_view(block_rows):
    return block_rows.reshape(block_rows.shape[0], HEADS, HEAD_DIM)


def group_probs(query_heads, key_heads):
    score_scale = 1.0 / math.sqrt(HEAD_DIM)
    scores = (
        jnp.einsum("qhd,khd->hqk", query_heads, key_heads, preferred_element_type=jnp.float32)
        * score_scale
    )
    top_score = jnp.max(scores, axis=-1, keepdims=True)
    expo_terms = jnp.exp(scores - top_score)
    return expo_terms / jnp.sum(expo_terms, axis=-1, keepdims=True)


def attend_layer(queries, key_rows, value_rows, out_grads):
    score_scale = 1.0 / math.sqrt(HEAD_DIM)
    per_group = HEADS // GROUPS
    query_heads = head_view(queries)
    key_heads = head_view(key_rows)
    value_heads = head_view(value_rows)
    grad_heads = head_view(out_grads)
    attended_out = []
    query_out = []
    key_out = []
    value_out = []
    for group_index in range(GROUPS):
        first_head = group_index * per_group
        last_head = first_head + per_group
        query_group = query_heads[:, first_head:last_head]
        key_group = key_heads[:, first_head:last_head]
        value_group = value_heads[:, first_head:last_head]
        grad_group = grad_heads[:, first_head:last_head]
        probs = group_probs(query_group, key_group)
        probs_low = probs.astype(jnp.bfloat16)
        attended_out.append(
            jnp.einsum(
                "hqk,khd->qhd", probs_low, value_group, preferred_element_type=jnp.float32
            ).astype(jnp.bfloat16)
        )
        grad_probs = jnp.einsum(
            "qhd,khd->hqk", grad_group, value_group, preferred_element_type=jnp.float32
        )
        row_dot = jnp.sum(probs * grad_probs, axis=-1, keepdims=True)
        grad_scores = (probs * (grad_probs - row_dot) * score_scale).astype(jnp.bfloat16)
        query_out.append(
            jnp.einsum(
                "hqk,khd->qhd", grad_scores, key_group, preferred_element_type=jnp.float32
            ).astype(jnp.bfloat16)
        )
        key_out.append(
            jnp.einsum(
                "hqk,qhd->khd", grad_scores, query_group, preferred_element_type=jnp.float32
            ).astype(jnp.bfloat16)
        )
        value_out.append(
            jnp.einsum(
                "hqk,qhd->khd", probs_low, grad_group, preferred_element_type=jnp.float32
            ).astype(jnp.bfloat16)
        )
    key_count = key_rows.shape[0]
    query_count = queries.shape[0]
    return (
        jnp.concatenate(attended_out, axis=1).reshape(query_count, FEATURES),
        jnp.concatenate(query_out, axis=1).reshape(query_count, FEATURES),
        jnp.concatenate(key_out, axis=1).reshape(key_count, FEATURES),
        jnp.concatenate(value_out, axis=1).reshape(key_count, FEATURES),
    )


def head_step(q, g, k_own, k_far, v_own, v_far):
    score_scale = 1.0 / math.sqrt(HEAD_DIM)

    def rows_dot(a, b):
        return lax.dot_general(a, b, (((1,), (1,)), ((), ())), preferred_element_type=jnp.float32)

    def dot(a, b):
        return lax.dot_general(a, b, (((1,), (0,)), ((), ())), preferred_element_type=jnp.float32)

    def cols_dot(a, b):
        return lax.dot_general(a, b, (((0,), (0,)), ((), ())), preferred_element_type=jnp.float32)

    s_own = rows_dot(q, k_own) * score_scale
    s_far = rows_dot(q, k_far) * score_scale
    top = jnp.maximum(
        jnp.max(s_own, axis=-1, keepdims=True), jnp.max(s_far, axis=-1, keepdims=True)
    )
    e_own = jnp.exp(s_own - top)
    e_far = jnp.exp(s_far - top)
    total = jnp.sum(e_own, axis=-1, keepdims=True) + jnp.sum(e_far, axis=-1, keepdims=True)
    inverse = 1.0 / total
    p_own = e_own * inverse
    p_far = e_far * inverse
    b_own = p_own.astype(jnp.bfloat16)
    b_far = p_far.astype(jnp.bfloat16)
    attended = dot(b_own, v_own) + dot(b_far, v_far)
    gp_own = rows_dot(g, v_own)
    gp_far = rows_dot(g, v_far)
    row_dot = jnp.sum(p_own * gp_own, axis=-1, keepdims=True) + jnp.sum(
        p_far * gp_far, axis=-1, keepdims=True
    )
    d_own = (p_own * (gp_own - row_dot) * score_scale).astype(jnp.bfloat16)
    d_far = (p_far * (gp_far - row_dot) * score_scale).astype(jnp.bfloat16)
    grad_query = dot(d_own, k_own) + dot(d_far, k_far)
    return (
        attended,
        grad_query,
        cols_dot(d_own, q),
        cols_dot(b_own, g),
        cols_dot(d_far, q),
        cols_dot(b_far, g),
    )


def fused_kernel(segments, devices, *refs):
    query, key, value, cotangent, order = refs[:5]
    passed_out, query_out, key_out, value_out = refs[5:9]
    heads = FEATURES // devices // HEAD_DIM
    full = refs[9 : 9 + heads]
    back, own_sum, far_sum, local_sem, in_s, in_r, back_s, back_r = refs[9 + heads :]
    segment = lax.axis_index("segment")
    seq = lax.axis_index("seq")
    chip = seq // 2
    core = seq % 2
    blocks = devices // 2
    width = FEATURES // devices
    group = seq * width // (FEATURES // GROUPS)
    after = (segment + 1) % segments
    before = (segment + segments - 1) % segments

    def chip_at(step):
        return 2 * ((chip // 2 + step // 2) % 2) + (chip + step) % 2

    def peer(step):
        return 2 * chip_at(step // 2) + (core + step) % 2

    def send(source, target, send_sem, recv_sem, device):
        copy = pltpu.make_async_remote_copy(
            src_ref=source, dst_ref=target, send_sem=send_sem, recv_sem=recv_sem,
            device_id=device, device_id_type=pl.DeviceIdType.MESH,
        )
        copy.start()
        return copy

    barrier = pltpu.get_barrier_semaphore()
    greeted = [(segment, peer(e)) for e in range(1, devices)]
    greeted += [(before, peer(e)) for e in range(devices)]
    for device in greeted:
        pl.semaphore_signal(barrier, inc=1, device_id=device, device_id_type=pl.DeviceIdType.MESH)

    def columns(device, head):
        return pl.ds(pl.multiple_of(device * width + head * HEAD_DIM, HEAD_DIM), HEAD_DIM)

    inputs = (query, key, value, cotangent)
    outputs = (passed_out, query_out, key_out, value_out)
    kept = [
        [
            pltpu.make_async_copy(
                ref.at[0, :, columns(seq, head)], full[head].at[index, chip, core],
                local_sem.at[head, index],
            )
            for index, ref in enumerate(inputs)
        ]
        for head in range(heads)
    ]
    for copy in sum(kept, []):
        copy.start()
    pl.semaphore_wait(barrier, len(greeted))

    arriving = []
    for head in range(heads):
        started = []
        for e in ORDER:
            for index, ref in enumerate(inputs):
                started.append(
                    send(ref.at[0, :, columns(peer(e), head)], full[head].at[index, chip, core],
                         in_s.at[head, index, e], in_r.at[head, index, e], (segment, peer(e)))
                )
        arriving.append(started)

    def compute(head):
        def rows(index, block):
            return full[head][index, block].reshape(BLOCK, HEAD_DIM)

        def step(block, carry):
            wanted = order[0, group, block]
            att, dq, dk, dv, fk, fv = head_step(
                rows(0, block), rows(3, block), rows(1, block), rows(1, wanted),
                rows(2, block), rows(2, wanted),
            )
            shape = (2, TOK_DEV, HEAD_DIM)
            back[head, 0, block] = att.astype(jnp.bfloat16).reshape(shape)
            back[head, 1, block] = dq.astype(jnp.bfloat16).reshape(shape)
            own_sum[0, block] = dk
            own_sum[1, block] = dv
            far_sum[0, block] = fk
            far_sum[1, block] = fv
            return carry

        lax.fori_loop(0, blocks, step, 0)

        def total(block, carry):
            asking = 0
            for b in range(blocks):
                asking = jnp.where(order[0, group, b] == block, b, asking)
            for which in range(2):
                summed = own_sum[which, block] + far_sum[which, asking]
                back[head, 2 + which, block] = summed.astype(jnp.bfloat16).reshape(
                    2, TOK_DEV, HEAD_DIM
                )
            return carry

        lax.fori_loop(0, blocks, total, 0)

    leaving = []
    for head in range(heads):
        for copy in kept[head]:
            copy.wait()
        for copy in arriving[head]:
            copy.wait_recv()
        compute(head)
        for index, out in enumerate(outputs):
            for e in (*ORDER, 0):
                source = back.at[head, index, chip_at(e // 2), (core + e) % 2]
                if index > 0 and e == 0:
                    out[0, :, columns(seq, head)] = back[head, index, chip, core]
                    continue
                leaving.append(
                    send(source, out.at[0, :, columns(seq, head)], back_s.at[head, index, e],
                         back_r.at[head, index, e], (segment if index else after, peer(e)))
                )
    for copy in leaving:
        copy.wait_recv()
    for copy in sum(arriving, []) + leaving:
        copy.wait_send()


def write_kernel(*refs):
    sems = refs[8]
    copies = [pltpu.make_async_copy(refs[i], refs[4 + i], sems.at[i]) for i in range(4)]
    for copy in copies:
        copy.start()
    for copy in copies:
        copy.wait()


def per_device_fused(query, key, value, cotangent, block_order):
    segments = lax.axis_size("segment")
    devices = lax.axis_size("seq")
    heads = FEATURES // devices // HEAD_DIM
    blocks = devices // 2
    low = jnp.bfloat16
    held = (4, blocks, 2, TOK_DEV, HEAD_DIM)
    sums = (2, blocks, BLOCK, HEAD_DIM)
    scratch = [pltpu.VMEM(held, low)] * heads + [pltpu.VMEM((heads, *held), low)]
    scratch += [pltpu.VMEM(sums, jnp.float32)] * 2
    scratch += [pltpu.SemaphoreType.DMA((heads, 4))]
    scratch += [pltpu.SemaphoreType.DMA((heads, 4, devices))] * 4
    whole = pl.BlockSpec(memory_space=pltpu.VMEM)
    out = jax.ShapeDtypeStruct(query.shape, low)
    outs = pl.pallas_call(
        functools.partial(fused_kernel, segments, devices),
        out_shape=(out,) * 4,
        in_specs=[pl.BlockSpec(memory_space=pltpu.HBM)] * 4
        + [pl.BlockSpec(memory_space=pltpu.SMEM)],
        out_specs=(whole,) * 4,
        scratch_shapes=scratch,
        compiler_params=pltpu.CompilerParams(
            collective_id=0, has_side_effects=True, vmem_limit_bytes=48 * 1024 * 1024
        ),
    )(*[pltpu.with_memory_space_constraint(x, pltpu.HBM) for x in (query, key, value, cotangent, block_order)])
    return pl.pallas_call(
        write_kernel,
        out_shape=(out,) * 4,
        in_specs=[pl.BlockSpec(memory_space=pl.ANY)] * 4,
        out_specs=(pl.BlockSpec(memory_space=pltpu.HBM),) * 4,
        scratch_shapes=[pltpu.SemaphoreType.DMA((4,))],
        compiler_params=pltpu.CompilerParams(vmem_limit_bytes=8 * 1024 * 1024),
    )(*outs)


def per_device_routed(query, key, value, cotangent, block_order):
    devices = lax.axis_size("seq")
    lower_half = lax.axis_index("seq") % 2 == 0
    both_halves, same_half, returning, summed_back = route_tables(block_order[0], devices)
    mine = jnp.stack([key[0], value[0]])
    swapped = partner_rows(mine)
    own_block = jnp.where(
        lower_half,
        jnp.concatenate([mine, swapped], axis=1),
        jnp.concatenate([swapped, mine], axis=1),
    )
    far_block = routed(mine[:, None], both_halves, GROUPS).reshape(2, BLOCK, FEATURES)
    key_sets = jnp.concatenate([own_block, far_block], axis=1)
    attended, grad_queries, key_part, value_part = attend_layer(
        query[0], key_sets[0], key_sets[1], cotangent[0]
    )
    passed_rows = from_behind(attended, "segment", 1)
    partials = jnp.stack([key_part, value_part])
    own_parts = partials[:, :BLOCK]
    far_parts = partials[:, BLOCK:].reshape(2, 2, TOK_DEV, FEATURES)
    kept = jnp.where(lower_half, own_parts[:, :TOK_DEV], own_parts[:, TOK_DEV:])
    given = jnp.where(lower_half, own_parts[:, TOK_DEV:], own_parts[:, :TOK_DEV])
    from_partner = partner_rows(given)
    returned = routed(far_parts, returning, GROUPS)
    matched_low = (returned[:, 0].astype(jnp.float32) + returned[:, 1].astype(jnp.float32)).astype(
        jnp.bfloat16
    )
    matched_terms = lax.optimization_barrier(matched_low).astype(jnp.float32)
    totals = (kept.astype(jnp.float32) + from_partner.astype(jnp.float32) + matched_terms).astype(
        jnp.bfloat16
    )
    return (passed_rows[None], grad_queries[None], totals[0][None], totals[1][None])


def solution(mesh):
    in_specs = (
        P("segment", "seq", None),
        P("segment", "seq", None),
        P("segment", "seq", None),
        P("segment", "seq", None),
        P("segment", None, None),
    )
    out_specs = (
        P("segment", "seq", None),
        P("segment", "seq", None),
        P("segment", "seq", None),
        P("segment", "seq", None),
    )
    fused = mesh.shape["seq"] == 8 and mesh.shape["segment"] > 1
    return jax.shard_map(
        per_device_fused if fused else per_device_routed, mesh=mesh, in_specs=in_specs, out_specs=out_specs, check_vma=False
    )
```

```python
import functools
import math

import jax
import jax.numpy as jnp
from jax import lax
from jax.experimental import pallas as pl
from jax.experimental.pallas import tpu as pltpu
from jax.sharding import PartitionSpec as P

HEADS = 16
HEAD_DIM = 128
GROUPS = 4
BLOCK = 256
TOK_DEV = 128
FEATURES = 2048
ORDER = (2, 4, 6, 3, 5, 7, 1)


def from_partner_2(shard, axis, bit):
    return lax.ppermute(shard, axis, [(i, i ^ 1 << bit) for i in range(lax.axis_size(axis))])


def from_behind(value, axis, steps):
    count = lax.axis_size(axis)
    pairs = [(source, (source + steps) % count) for source in range(count)]
    return lax.ppermute(value, axis, pairs)


def partner_rows(stacked):
    return from_partner_2(stacked, "seq", 0)


def chosen(slots, wanted):
    mask = (wanted[:, None] == jnp.arange(slots.shape[1])[None, :]).astype(slots.dtype)
    return jnp.einsum(
        "ts,csrw->ctrw", mask, slots, preferred_element_type=jnp.float32
    ).astype(slots.dtype)


def routed(stacked, table, group_count):
    devices = lax.axis_size("seq")
    channels, slot_count, row_count, width = stacked.shape
    piece_rows = row_count // devices
    pieces = stacked.reshape(channels, slot_count, devices, piece_rows * width)
    arrived = lax.all_to_all(pieces, "seq", split_axis=2, concat_axis=2, tiled=True)
    arrived = arrived.reshape(
        channels, slot_count * devices, piece_rows, group_count, width // group_count
    )
    picked = [
        chosen(arrived[:, :, :, group_index, :], table[group_index])
        for group_index in range(group_count)
    ]
    fanout = table.shape[1] // devices
    outward = jnp.stack(picked, axis=3).reshape(channels, fanout, devices, piece_rows * width)
    landed = lax.all_to_all(outward, "seq", split_axis=2, concat_axis=2, tiled=True)
    return landed.reshape(channels, fanout, row_count, width)


def route_tables(order, devices):
    device_ids = jnp.arange(devices, dtype=jnp.int32)
    half_ids = jnp.arange(2, dtype=jnp.int32)
    group_count = order.shape[0]
    target = jnp.take(order, device_ids // 2, axis=1)
    both_halves = (2 * target[:, None, :] + half_ids[None, :, None]).reshape(
        group_count, 2 * devices
    )
    same_half = 2 * target + device_ids % 2
    inverse = jnp.argsort(order, axis=1)
    asking = 2 * jnp.take(inverse, device_ids // 2, axis=1)
    returning = (
        (device_ids % 2)[None, None, :] * devices + asking[:, None, :] + half_ids[None, :, None]
    ).reshape(group_count, 2 * devices)
    summed_back = asking + device_ids % 2
    return (both_halves, same_half, returning, summed_back)


def head_view(block_rows):
    return block_rows.reshape(block_rows.shape[0], HEADS, HEAD_DIM)


def group_probs(query_heads, key_heads):
    score_scale = 1.0 / math.sqrt(HEAD_DIM)
    scores = (
        jnp.einsum("qhd,khd->hqk", query_heads, key_heads, preferred_element_type=jnp.float32)
        * score_scale
    )
    top_score = jnp.max(scores, axis=-1, keepdims=True)
    expo_terms = jnp.exp(scores - top_score)
    return expo_terms / jnp.sum(expo_terms, axis=-1, keepdims=True)


def attend_layer(queries, key_rows, value_rows, out_grads):
    score_scale = 1.0 / math.sqrt(HEAD_DIM)
    per_group = HEADS // GROUPS
    query_heads = head_view(queries)
    key_heads = head_view(key_rows)
    value_heads = head_view(value_rows)
    grad_heads = head_view(out_grads)
    attended_out = []
    query_out = []
    key_out = []
    value_out = []
    for group_index in range(GROUPS):
        first_head = group_index * per_group
        last_head = first_head + per_group
        query_group = query_heads[:, first_head:last_head]
        key_group = key_heads[:, first_head:last_head]
        value_group = value_heads[:, first_head:last_head]
        grad_group = grad_heads[:, first_head:last_head]
        probs = group_probs(query_group, key_group)
        probs_low = probs.astype(jnp.bfloat16)
        attended_out.append(
            jnp.einsum(
                "hqk,khd->qhd", probs_low, value_group, preferred_element_type=jnp.float32
            ).astype(jnp.bfloat16)
        )
        grad_probs = jnp.einsum(
            "qhd,khd->hqk", grad_group, value_group, preferred_element_type=jnp.float32
        )
        row_dot = jnp.sum(probs * grad_probs, axis=-1, keepdims=True)
        grad_scores = (probs * (grad_probs - row_dot) * score_scale).astype(jnp.bfloat16)
        query_out.append(
            jnp.einsum(
                "hqk,khd->qhd", grad_scores, key_group, preferred_element_type=jnp.float32
            ).astype(jnp.bfloat16)
        )
        key_out.append(
            jnp.einsum(
                "hqk,qhd->khd", grad_scores, query_group, preferred_element_type=jnp.float32
            ).astype(jnp.bfloat16)
        )
        value_out.append(
            jnp.einsum(
                "hqk,qhd->khd", probs_low, grad_group, preferred_element_type=jnp.float32
            ).astype(jnp.bfloat16)
        )
    key_count = key_rows.shape[0]
    query_count = queries.shape[0]
    return (
        jnp.concatenate(attended_out, axis=1).reshape(query_count, FEATURES),
        jnp.concatenate(query_out, axis=1).reshape(query_count, FEATURES),
        jnp.concatenate(key_out, axis=1).reshape(key_count, FEATURES),
        jnp.concatenate(value_out, axis=1).reshape(key_count, FEATURES),
    )


def head_step(q, g, k_own, k_far, v_own, v_far):
    score_scale = 1.0 / math.sqrt(HEAD_DIM)

    def rows_dot(a, b):
        return lax.dot_general(a, b, (((1,), (1,)), ((), ())), preferred_element_type=jnp.float32)

    def dot(a, b):
        return lax.dot_general(a, b, (((1,), (0,)), ((), ())), preferred_element_type=jnp.float32)

    def cols_dot(a, b):
        return lax.dot_general(a, b, (((0,), (0,)), ((), ())), preferred_element_type=jnp.float32)

    s_own = rows_dot(q, k_own) * score_scale
    s_far = rows_dot(q, k_far) * score_scale
    top = jnp.maximum(
        jnp.max(s_own, axis=-1, keepdims=True), jnp.max(s_far, axis=-1, keepdims=True)
    )
    e_own = jnp.exp(s_own - top)
    e_far = jnp.exp(s_far - top)
    total = jnp.sum(e_own, axis=-1, keepdims=True) + jnp.sum(e_far, axis=-1, keepdims=True)
    inverse = 1.0 / total
    p_own = e_own * inverse
    p_far = e_far * inverse
    b_own = p_own.astype(jnp.bfloat16)
    b_far = p_far.astype(jnp.bfloat16)
    attended = dot(b_own, v_own) + dot(b_far, v_far)
    gp_own = rows_dot(g, v_own)
    gp_far = rows_dot(g, v_far)
    row_dot = jnp.sum(p_own * gp_own, axis=-1, keepdims=True) + jnp.sum(
        p_far * gp_far, axis=-1, keepdims=True
    )
    d_own = (p_own * (gp_own - row_dot) * score_scale).astype(jnp.bfloat16)
    d_far = (p_far * (gp_far - row_dot) * score_scale).astype(jnp.bfloat16)
    grad_query = dot(d_own, k_own) + dot(d_far, k_far)
    return (
        attended,
        grad_query,
        cols_dot(d_own, q),
        cols_dot(b_own, g),
        cols_dot(d_far, q),
        cols_dot(b_far, g),
    )


def fused_kernel(segments, devices, *refs):
    query, key, value, cotangent, block_order = refs[:5]
    passed_out, query_out, key_out, value_out = refs[5:9]
    heads = FEATURES // devices // HEAD_DIM
    full = refs[9 : 9 + heads]
    (back, own_sum, far_sum, order, order_sem, in_s, in_r, passed_s, grad_s, out_r,
     next_in) = refs[9 + heads :]
    segment = lax.axis_index("segment")
    seq = lax.axis_index("seq")
    chip = seq // 2
    core = seq % 2
    blocks = devices // 2
    width = FEATURES // devices
    group = seq * width // (FEATURES // GROUPS)
    after = (segment + 1) % segments
    before = (segment + segments - 1) % segments

    def peer(step):
        other = 2 * ((chip // 2 + step // 4) % 2) + (chip + step // 2) % 2
        return 2 * other + (core + step) % 2

    def send(source, target, send_sem, recv_sem, device):
        pltpu.make_async_remote_copy(
            src_ref=source, dst_ref=target, send_sem=send_sem, recv_sem=recv_sem,
            device_id=device, device_id_type=pl.DeviceIdType.MESH,
        ).start()

    def signal(sem, device):
        pl.semaphore_signal(sem, inc=1, device_id=device, device_id_type=pl.DeviceIdType.MESH)

    def take(ref, sem):
        pltpu.make_async_copy(ref, ref, sem).wait()

    barrier = pltpu.get_barrier_semaphore()
    for e in range(1, devices):
        signal(barrier, (segment, peer(e)))

    @pl.when(segment < segments - 1)
    def _():
        signal(barrier, (after, seq))

    def columns(device, head):
        return pl.ds(pl.multiple_of(device * width + head * HEAD_DIM, HEAD_DIM), HEAD_DIM)

    inputs = (query, key, value, cotangent)
    outputs = (passed_out, query_out, key_out, value_out)
    pltpu.make_async_copy(block_order, order, order_sem.at[0]).start()
    for head in range(heads):
        for index, ref in enumerate(inputs):
            pltpu.make_async_copy(
                ref.at[0, :, columns(seq, head)], full[head].at[index, seq], in_r.at[head]
            ).start()
    first, last = segment == 0, segment == segments - 1
    pl.semaphore_wait(barrier, devices - jnp.where(first, 1, 0) + jnp.where(last, 1, 0))

    for head in range(heads):
        for e in ORDER:
            for index, ref in enumerate(inputs):
                send(ref.at[0, :, columns(peer(e), head)], full[head].at[index, seq],
                     in_s.at[0], in_r.at[head], (segment, peer(e)))

    @pl.when(first)
    def _():
        signal(barrier, (before, seq))

    @pl.when(segment > 0)
    def _():
        signal(next_in, (before, seq))

    def compute(head):
        def rows(index, block):
            return full[head][index, pl.ds(2 * block, 2)].reshape(BLOCK, HEAD_DIM)

        def step(block, carry):
            wanted = order[0, group, block]
            att, dq, dk, dv, fk, fv = head_step(
                rows(0, block), rows(3, block), rows(1, block), rows(1, wanted),
                rows(2, block), rows(2, wanted),
            )
            shape = (2, TOK_DEV, HEAD_DIM)
            both = pl.ds(2 * block, 2)
            back[4 * head, both] = att.astype(jnp.bfloat16).reshape(shape)
            back[4 * head + 1, both] = dq.astype(jnp.bfloat16).reshape(shape)
            own_sum[0, block] = dk
            own_sum[1, block] = dv
            far_sum[0, block] = fk
            far_sum[1, block] = fv
            return carry

        lax.fori_loop(0, blocks, step, 0)

        def total(block, carry):
            asking = 0
            for b in range(blocks):
                asking = jnp.where(order[0, group, b] == block, b, asking)
            for which in range(2):
                summed = own_sum[which, block] + far_sum[which, asking]
                back[4 * head + 2 + which, pl.ds(2 * block, 2)] = summed.astype(
                    jnp.bfloat16
                ).reshape(2, TOK_DEV, HEAD_DIM)
            return carry

        lax.fori_loop(0, blocks, total, 0)

    for head in range(heads):
        if head == 0:
            take(order.at[...], order_sem.at[0])
        take(full[head], in_r.at[head])
        compute(head)
        if head == 0:
            @pl.when(segment < segments - 1)
            def _():
                pl.semaphore_wait(next_in, 1)

        for index, out in enumerate(outputs):
            for e in (*ORDER, 0):
                source = back.at[4 * head + index, peer(e)]
                target = out.at[0, :, columns(seq, head)]
                if index == 0:
                    send(source, target, passed_s.at[0], out_r.at[0], (after, peer(e)))
                elif e:
                    send(source, target, grad_s.at[0], out_r.at[0], (segment, peer(e)))
                else:
                    pltpu.make_async_copy(source, target, out_r.at[0]).start()
    gone = devices - 1
    take(back.at[:, pl.ds(0, gone)], in_s.at[0])
    take(back, out_r.at[0])
    take(back.at[pl.ds(0, heads)], passed_s.at[0])
    take(back.at[pl.ds(0, 3 * heads), pl.ds(0, gone)], grad_s.at[0])


def write_kernel(*refs):
    sems = refs[8]
    copies = [pltpu.make_async_copy(refs[i], refs[4 + i], sems.at[i]) for i in range(4)]
    for copy in copies:
        copy.start()
    for copy in copies:
        copy.wait()


def per_device_fused(query, key, value, cotangent, block_order):
    segments = lax.axis_size("segment")
    devices = lax.axis_size("seq")
    heads = FEATURES // devices // HEAD_DIM
    blocks = devices // 2
    low = jnp.bfloat16
    held = (4, devices, TOK_DEV, HEAD_DIM)
    sums = (2, blocks, BLOCK, HEAD_DIM)
    scratch = [pltpu.VMEM(held, low)] * heads
    scratch += [pltpu.VMEM((4 * heads, *held[1:]), low)]
    scratch += [pltpu.VMEM(sums, jnp.float32)] * 2
    scratch += [pltpu.SMEM(block_order.shape, jnp.int32), pltpu.SemaphoreType.DMA((1,))]
    scratch += [pltpu.SemaphoreType.DMA((1,)), pltpu.SemaphoreType.DMA((heads,))]
    scratch += [pltpu.SemaphoreType.DMA((1,))] * 3 + [pltpu.SemaphoreType.REGULAR]
    whole = pl.BlockSpec(memory_space=pltpu.VMEM)
    out = jax.ShapeDtypeStruct(query.shape, low)
    outs = pl.pallas_call(
        functools.partial(fused_kernel, segments, devices),
        out_shape=(out,) * 4,
        in_specs=[pl.BlockSpec(memory_space=pltpu.HBM)] * 5,
        out_specs=(whole,) * 4,
        scratch_shapes=scratch,
        compiler_params=pltpu.CompilerParams(
            collective_id=0, has_side_effects=True, vmem_limit_bytes=48 * 1024 * 1024
        ),
    )(*[pltpu.with_memory_space_constraint(x, pltpu.HBM) for x in (query, key, value, cotangent, block_order)])
    return pl.pallas_call(
        write_kernel,
        out_shape=(out,) * 4,
        in_specs=[pl.BlockSpec(memory_space=pl.ANY)] * 4,
        out_specs=(pl.BlockSpec(memory_space=pltpu.HBM),) * 4,
        scratch_shapes=[pltpu.SemaphoreType.DMA((4,))],
        compiler_params=pltpu.CompilerParams(vmem_limit_bytes=8 * 1024 * 1024),
    )(*outs)


def per_device_routed(query, key, value, cotangent, block_order):
    devices = lax.axis_size("seq")
    lower_half = lax.axis_index("seq") % 2 == 0
    both_halves, same_half, returning, summed_back = route_tables(block_order[0], devices)
    mine = jnp.stack([key[0], value[0]])
    swapped = partner_rows(mine)
    own_block = jnp.where(
        lower_half,
        jnp.concatenate([mine, swapped], axis=1),
        jnp.concatenate([swapped, mine], axis=1),
    )
    far_block = routed(mine[:, None], both_halves, GROUPS).reshape(2, BLOCK, FEATURES)
    key_sets = jnp.concatenate([own_block, far_block], axis=1)
    attended, grad_queries, key_part, value_part = attend_layer(
        query[0], key_sets[0], key_sets[1], cotangent[0]
    )
    passed_rows = from_behind(attended, "segment", 1)
    partials = jnp.stack([key_part, value_part])
    own_parts = partials[:, :BLOCK]
    far_parts = partials[:, BLOCK:].reshape(2, 2, TOK_DEV, FEATURES)
    kept = jnp.where(lower_half, own_parts[:, :TOK_DEV], own_parts[:, TOK_DEV:])
    given = jnp.where(lower_half, own_parts[:, TOK_DEV:], own_parts[:, :TOK_DEV])
    from_partner = partner_rows(given)
    returned = routed(far_parts, returning, GROUPS)
    matched_low = (returned[:, 0].astype(jnp.float32) + returned[:, 1].astype(jnp.float32)).astype(
        jnp.bfloat16
    )
    matched_terms = lax.optimization_barrier(matched_low).astype(jnp.float32)
    totals = (kept.astype(jnp.float32) + from_partner.astype(jnp.float32) + matched_terms).astype(
        jnp.bfloat16
    )
    return (passed_rows[None], grad_queries[None], totals[0][None], totals[1][None])


def solution(mesh):
    in_specs = (
        P("segment", "seq", None),
        P("segment", "seq", None),
        P("segment", "seq", None),
        P("segment", "seq", None),
        P("segment", None, None),
    )
    out_specs = (
        P("segment", "seq", None),
        P("segment", "seq", None),
        P("segment", "seq", None),
        P("segment", "seq", None),
    )
    fused = mesh.shape["seq"] == 8 and mesh.shape["segment"] > 1
    return jax.shard_map(
        per_device_fused if fused else per_device_routed, mesh=mesh, in_specs=in_specs, out_specs=out_specs, check_vma=False
    )
```

```python
import functools
import math

import jax
import jax.numpy as jnp
from jax import lax
from jax.experimental import pallas as pl
from jax.experimental.pallas import tpu as pltpu
from jax.sharding import PartitionSpec as P

HEADS = 16
HEAD_DIM = 128
GROUPS = 4
BLOCK = 256
TOK_DEV = 128
FEATURES = 2048
ORDER = (2, 4, 6, 3, 5, 7, 1)


def from_partner_2(shard, axis, bit):
    return lax.ppermute(shard, axis, [(i, i ^ 1 << bit) for i in range(lax.axis_size(axis))])


def from_behind(value, axis, steps):
    count = lax.axis_size(axis)
    pairs = [(source, (source + steps) % count) for source in range(count)]
    return lax.ppermute(value, axis, pairs)


def partner_rows(stacked):
    return from_partner_2(stacked, "seq", 0)


def chosen(slots, wanted):
    mask = (wanted[:, None] == jnp.arange(slots.shape[1])[None, :]).astype(slots.dtype)
    return jnp.einsum(
        "ts,csrw->ctrw", mask, slots, preferred_element_type=jnp.float32
    ).astype(slots.dtype)


def routed(stacked, table, group_count):
    devices = lax.axis_size("seq")
    channels, slot_count, row_count, width = stacked.shape
    piece_rows = row_count // devices
    pieces = stacked.reshape(channels, slot_count, devices, piece_rows * width)
    arrived = lax.all_to_all(pieces, "seq", split_axis=2, concat_axis=2, tiled=True)
    arrived = arrived.reshape(
        channels, slot_count * devices, piece_rows, group_count, width // group_count
    )
    picked = [
        chosen(arrived[:, :, :, group_index, :], table[group_index])
        for group_index in range(group_count)
    ]
    fanout = table.shape[1] // devices
    outward = jnp.stack(picked, axis=3).reshape(channels, fanout, devices, piece_rows * width)
    landed = lax.all_to_all(outward, "seq", split_axis=2, concat_axis=2, tiled=True)
    return landed.reshape(channels, fanout, row_count, width)


def route_tables(order, devices):
    device_ids = jnp.arange(devices, dtype=jnp.int32)
    half_ids = jnp.arange(2, dtype=jnp.int32)
    group_count = order.shape[0]
    target = jnp.take(order, device_ids // 2, axis=1)
    both_halves = (2 * target[:, None, :] + half_ids[None, :, None]).reshape(
        group_count, 2 * devices
    )
    same_half = 2 * target + device_ids % 2
    inverse = jnp.argsort(order, axis=1)
    asking = 2 * jnp.take(inverse, device_ids // 2, axis=1)
    returning = (
        (device_ids % 2)[None, None, :] * devices + asking[:, None, :] + half_ids[None, :, None]
    ).reshape(group_count, 2 * devices)
    summed_back = asking + device_ids % 2
    return (both_halves, same_half, returning, summed_back)


def head_view(block_rows):
    return block_rows.reshape(block_rows.shape[0], HEADS, HEAD_DIM)


def group_probs(query_heads, key_heads):
    score_scale = 1.0 / math.sqrt(HEAD_DIM)
    scores = (
        jnp.einsum("qhd,khd->hqk", query_heads, key_heads, preferred_element_type=jnp.float32)
        * score_scale
    )
    top_score = jnp.max(scores, axis=-1, keepdims=True)
    expo_terms = jnp.exp(scores - top_score)
    return expo_terms / jnp.sum(expo_terms, axis=-1, keepdims=True)


def attend_layer(queries, key_rows, value_rows, out_grads):
    score_scale = 1.0 / math.sqrt(HEAD_DIM)
    per_group = HEADS // GROUPS
    query_heads = head_view(queries)
    key_heads = head_view(key_rows)
    value_heads = head_view(value_rows)
    grad_heads = head_view(out_grads)
    attended_out = []
    query_out = []
    key_out = []
    value_out = []
    for group_index in range(GROUPS):
        first_head = group_index * per_group
        last_head = first_head + per_group
        query_group = query_heads[:, first_head:last_head]
        key_group = key_heads[:, first_head:last_head]
        value_group = value_heads[:, first_head:last_head]
        grad_group = grad_heads[:, first_head:last_head]
        probs = group_probs(query_group, key_group)
        probs_low = probs.astype(jnp.bfloat16)
        attended_out.append(
            jnp.einsum(
                "hqk,khd->qhd", probs_low, value_group, preferred_element_type=jnp.float32
            ).astype(jnp.bfloat16)
        )
        grad_probs = jnp.einsum(
            "qhd,khd->hqk", grad_group, value_group, preferred_element_type=jnp.float32
        )
        row_dot = jnp.sum(probs * grad_probs, axis=-1, keepdims=True)
        grad_scores = (probs * (grad_probs - row_dot) * score_scale).astype(jnp.bfloat16)
        query_out.append(
            jnp.einsum(
                "hqk,khd->qhd", grad_scores, key_group, preferred_element_type=jnp.float32
            ).astype(jnp.bfloat16)
        )
        key_out.append(
            jnp.einsum(
                "hqk,qhd->khd", grad_scores, query_group, preferred_element_type=jnp.float32
            ).astype(jnp.bfloat16)
        )
        value_out.append(
            jnp.einsum(
                "hqk,qhd->khd", probs_low, grad_group, preferred_element_type=jnp.float32
            ).astype(jnp.bfloat16)
        )
    key_count = key_rows.shape[0]
    query_count = queries.shape[0]
    return (
        jnp.concatenate(attended_out, axis=1).reshape(query_count, FEATURES),
        jnp.concatenate(query_out, axis=1).reshape(query_count, FEATURES),
        jnp.concatenate(key_out, axis=1).reshape(key_count, FEATURES),
        jnp.concatenate(value_out, axis=1).reshape(key_count, FEATURES),
    )


def head_step(q, g, k_own, k_far, v_own, v_far):
    score_scale = 1.0 / math.sqrt(HEAD_DIM)

    def rows_dot(a, b):
        return lax.dot_general(a, b, (((1,), (1,)), ((), ())), preferred_element_type=jnp.float32)

    def dot(a, b):
        return lax.dot_general(a, b, (((1,), (0,)), ((), ())), preferred_element_type=jnp.float32)

    def cols_dot(a, b):
        return lax.dot_general(a, b, (((0,), (0,)), ((), ())), preferred_element_type=jnp.float32)

    s_own = rows_dot(q, k_own) * score_scale
    s_far = rows_dot(q, k_far) * score_scale
    top = jnp.maximum(
        jnp.max(s_own, axis=-1, keepdims=True), jnp.max(s_far, axis=-1, keepdims=True)
    )
    e_own = jnp.exp(s_own - top)
    e_far = jnp.exp(s_far - top)
    total = jnp.sum(e_own, axis=-1, keepdims=True) + jnp.sum(e_far, axis=-1, keepdims=True)
    inverse = 1.0 / total
    p_own = e_own * inverse
    p_far = e_far * inverse
    b_own = p_own.astype(jnp.bfloat16)
    b_far = p_far.astype(jnp.bfloat16)
    attended = dot(b_own, v_own) + dot(b_far, v_far)
    gp_own = rows_dot(g, v_own)
    gp_far = rows_dot(g, v_far)
    row_dot = jnp.sum(p_own * gp_own, axis=-1, keepdims=True) + jnp.sum(
        p_far * gp_far, axis=-1, keepdims=True
    )
    d_own = (p_own * (gp_own - row_dot) * score_scale).astype(jnp.bfloat16)
    d_far = (p_far * (gp_far - row_dot) * score_scale).astype(jnp.bfloat16)
    grad_query = dot(d_own, k_own) + dot(d_far, k_far)
    return (
        attended,
        grad_query,
        cols_dot(d_own, q),
        cols_dot(b_own, g),
        cols_dot(d_far, q),
        cols_dot(b_far, g),
    )


def fused_kernel(segments, devices, *refs):
    query, key, value, cotangent, block_order = refs[:5]
    passed_out, query_out, key_out, value_out = refs[5:9]
    heads = FEATURES // devices // HEAD_DIM
    full = refs[9 : 9 + heads]
    (back, own_sum, far_sum, order, order_sem, in_s, in_r, passed_s, grad_s, out_r,
     next_in) = refs[9 + heads :]
    segment = lax.axis_index("segment")
    seq = lax.axis_index("seq")
    chip = seq // 2
    core = seq % 2
    blocks = devices // 2
    width = FEATURES // devices
    group = seq * width // (FEATURES // GROUPS)
    after = (segment + 1) % segments
    before = (segment + segments - 1) % segments

    def peer(step):
        other = 2 * ((chip // 2 + step // 4) % 2) + (chip + step // 2) % 2
        return 2 * other + (core + step) % 2

    def send(source, target, send_sem, recv_sem, device):
        pltpu.make_async_remote_copy(
            src_ref=source, dst_ref=target, send_sem=send_sem, recv_sem=recv_sem,
            device_id=device, device_id_type=pl.DeviceIdType.MESH,
        ).start()

    def signal(sem, device):
        pl.semaphore_signal(sem, inc=1, device_id=device, device_id_type=pl.DeviceIdType.MESH)

    def take(ref, sem):
        pltpu.make_async_copy(ref, ref, sem).wait()

    barrier = pltpu.get_barrier_semaphore()
    for e in (*reversed(range(2, devices)), 1):
        signal(barrier, (segment, peer(e)))

    @pl.when(segment < segments - 1)
    def _():
        signal(barrier, (after, seq))

    def columns(device, head):
        return pl.ds(pl.multiple_of(device * width + head * HEAD_DIM, HEAD_DIM), HEAD_DIM)

    inputs = (query, key, value, cotangent)
    outputs = (passed_out, query_out, key_out, value_out)
    pltpu.make_async_copy(block_order, order, order_sem.at[0]).start()
    first, last = segment == 0, segment == segments - 1
    pl.semaphore_wait(barrier, devices - jnp.where(first, 1, 0) + jnp.where(last, 1, 0))

    for head in range(heads):
        for index, ref in enumerate(inputs):
            for e in ORDER:
                send(ref.at[0, :, columns(peer(e), head)], full[head].at[index, seq],
                     in_s.at[0], in_r.at[head], (segment, peer(e)))

    for head in range(heads):
        for index, ref in enumerate(inputs):
            pltpu.make_async_copy(
                ref.at[0, :, columns(seq, head)], full[head].at[index, seq], in_r.at[head]
            ).start()
    @pl.when(first)
    def _():
        signal(barrier, (before, seq))

    @pl.when(segment > 0)
    def _():
        signal(next_in, (before, seq))

    def compute(head):
        def rows(index, block):
            return full[head][index, pl.ds(2 * block, 2)].reshape(BLOCK, HEAD_DIM)

        def step(block, carry):
            wanted = order[0, group, block]
            att, dq, dk, dv, fk, fv = head_step(
                rows(0, block), rows(3, block), rows(1, block), rows(1, wanted),
                rows(2, block), rows(2, wanted),
            )
            shape = (2, TOK_DEV, HEAD_DIM)
            both = pl.ds(2 * block, 2)
            back[4 * head, both] = att.astype(jnp.bfloat16).reshape(shape)
            back[4 * head + 1, both] = dq.astype(jnp.bfloat16).reshape(shape)
            own_sum[0, block] = dk
            own_sum[1, block] = dv
            far_sum[0, block] = fk
            far_sum[1, block] = fv
            return carry

        lax.fori_loop(0, blocks, step, 0)

        def total(block, carry):
            asking = 0
            for b in range(blocks):
                asking = jnp.where(order[0, group, b] == block, b, asking)
            for which in range(2):
                summed = own_sum[which, block] + far_sum[which, asking]
                back[4 * head + 2 + which, pl.ds(2 * block, 2)] = summed.astype(
                    jnp.bfloat16
                ).reshape(2, TOK_DEV, HEAD_DIM)
            return carry

        lax.fori_loop(0, blocks, total, 0)

    for head in range(heads):
        if head == 0:
            take(order.at[...], order_sem.at[0])
        take(full[head], in_r.at[head])
        compute(head)
        if head == 0:
            @pl.when(segment < segments - 1)
            def _():
                pl.semaphore_wait(next_in, 1)

        for index, out in enumerate(outputs):
            for e in (*ORDER, 0):
                source = back.at[4 * head + index, peer(e)]
                target = out.at[0, :, columns(seq, head)]
                if index == 0:
                    send(source, target, passed_s.at[0], out_r.at[0], (after, peer(e)))
                elif e:
                    send(source, target, grad_s.at[0], out_r.at[0], (segment, peer(e)))
                else:
                    pltpu.make_async_copy(source, target, out_r.at[0]).start()
    gone = devices - 1
    take(back.at[:, pl.ds(0, gone)], in_s.at[0])
    take(back, out_r.at[0])
    take(back.at[pl.ds(0, heads)], passed_s.at[0])
    take(back.at[pl.ds(0, 3 * heads), pl.ds(0, gone)], grad_s.at[0])


def write_kernel(*refs):
    sems = refs[8]
    copies = [pltpu.make_async_copy(refs[i], refs[4 + i], sems.at[i]) for i in range(4)]
    for copy in copies:
        copy.start()
    for copy in copies:
        copy.wait()


def per_device_fused(query, key, value, cotangent, block_order):
    segments = lax.axis_size("segment")
    devices = lax.axis_size("seq")
    heads = FEATURES // devices // HEAD_DIM
    blocks = devices // 2
    low = jnp.bfloat16
    held = (4, devices, TOK_DEV, HEAD_DIM)
    sums = (2, blocks, BLOCK, HEAD_DIM)
    scratch = [pltpu.VMEM(held, low)] * heads
    scratch += [pltpu.VMEM((4 * heads, *held[1:]), low)]
    scratch += [pltpu.VMEM(sums, jnp.float32)] * 2
    scratch += [pltpu.SMEM(block_order.shape, jnp.int32), pltpu.SemaphoreType.DMA((1,))]
    scratch += [pltpu.SemaphoreType.DMA((1,)), pltpu.SemaphoreType.DMA((heads,))]
    scratch += [pltpu.SemaphoreType.DMA((1,))] * 3 + [pltpu.SemaphoreType.REGULAR]
    whole = pl.BlockSpec(memory_space=pltpu.VMEM)
    out = jax.ShapeDtypeStruct(query.shape, low)
    outs = pl.pallas_call(
        functools.partial(fused_kernel, segments, devices),
        out_shape=(out,) * 4,
        in_specs=[pl.BlockSpec(memory_space=pltpu.HBM)] * 5,
        out_specs=(whole,) * 4,
        scratch_shapes=scratch,
        compiler_params=pltpu.CompilerParams(
            collective_id=0, has_side_effects=True, vmem_limit_bytes=48 * 1024 * 1024
        ),
    )(*[pltpu.with_memory_space_constraint(x, pltpu.HBM) for x in (query, key, value, cotangent, block_order)])
    return pl.pallas_call(
        write_kernel,
        out_shape=(out,) * 4,
        in_specs=[pl.BlockSpec(memory_space=pl.ANY)] * 4,
        out_specs=(pl.BlockSpec(memory_space=pltpu.HBM),) * 4,
        scratch_shapes=[pltpu.SemaphoreType.DMA((4,))],
        compiler_params=pltpu.CompilerParams(vmem_limit_bytes=8 * 1024 * 1024),
    )(*outs)


def per_device_routed(query, key, value, cotangent, block_order):
    devices = lax.axis_size("seq")
    lower_half = lax.axis_index("seq") % 2 == 0
    both_halves, same_half, returning, summed_back = route_tables(block_order[0], devices)
    mine = jnp.stack([key[0], value[0]])
    swapped = partner_rows(mine)
    own_block = jnp.where(
        lower_half,
        jnp.concatenate([mine, swapped], axis=1),
        jnp.concatenate([swapped, mine], axis=1),
    )
    far_block = routed(mine[:, None], both_halves, GROUPS).reshape(2, BLOCK, FEATURES)
    key_sets = jnp.concatenate([own_block, far_block], axis=1)
    attended, grad_queries, key_part, value_part = attend_layer(
        query[0], key_sets[0], key_sets[1], cotangent[0]
    )
    passed_rows = from_behind(attended, "segment", 1)
    partials = jnp.stack([key_part, value_part])
    own_parts = partials[:, :BLOCK]
    far_parts = partials[:, BLOCK:].reshape(2, 2, TOK_DEV, FEATURES)
    kept = jnp.where(lower_half, own_parts[:, :TOK_DEV], own_parts[:, TOK_DEV:])
    given = jnp.where(lower_half, own_parts[:, TOK_DEV:], own_parts[:, :TOK_DEV])
    from_partner = partner_rows(given)
    returned = routed(far_parts, returning, GROUPS)
    matched_low = (returned[:, 0].astype(jnp.float32) + returned[:, 1].astype(jnp.float32)).astype(
        jnp.bfloat16
    )
    matched_terms = lax.optimization_barrier(matched_low).astype(jnp.float32)
    totals = (kept.astype(jnp.float32) + from_partner.astype(jnp.float32) + matched_terms).astype(
        jnp.bfloat16
    )
    return (passed_rows[None], grad_queries[None], totals[0][None], totals[1][None])


def solution(mesh):
    in_specs = (
        P("segment", "seq", None),
        P("segment", "seq", None),
        P("segment", "seq", None),
        P("segment", "seq", None),
        P("segment", None, None),
    )
    out_specs = (
        P("segment", "seq", None),
        P("segment", "seq", None),
        P("segment", "seq", None),
        P("segment", "seq", None),
    )
    fused = mesh.shape["seq"] == 8 and mesh.shape["segment"] > 1
    return jax.shard_map(
        per_device_fused if fused else per_device_routed, mesh=mesh, in_specs=in_specs, out_specs=out_specs, check_vma=False
    )
```

```python
import functools
import math

import jax
import jax.numpy as jnp
from jax import lax
from jax.experimental import pallas as pl
from jax.experimental.pallas import tpu as pltpu
from jax.sharding import PartitionSpec as P

HEADS = 16
HEAD_DIM = 128
GROUPS = 4
BLOCK = 256
TOK_DEV = 128
FEATURES = 2048
ORDER = (4, 2, 6, 5, 3, 7, 1)
NEAR = (2, 4, 3, 5)
EARLY = 1


def from_partner_2(shard, axis, bit):
    return lax.ppermute(shard, axis, [(i, i ^ 1 << bit) for i in range(lax.axis_size(axis))])


def from_behind(value, axis, steps):
    count = lax.axis_size(axis)
    pairs = [(source, (source + steps) % count) for source in range(count)]
    return lax.ppermute(value, axis, pairs)


def partner_rows(stacked):
    return from_partner_2(stacked, "seq", 0)


def chosen(slots, wanted):
    mask = (wanted[:, None] == jnp.arange(slots.shape[1])[None, :]).astype(slots.dtype)
    return jnp.einsum(
        "ts,csrw->ctrw", mask, slots, preferred_element_type=jnp.float32
    ).astype(slots.dtype)


def routed(stacked, table, group_count):
    devices = lax.axis_size("seq")
    channels, slot_count, row_count, width = stacked.shape
    piece_rows = row_count // devices
    pieces = stacked.reshape(channels, slot_count, devices, piece_rows * width)
    arrived = lax.all_to_all(pieces, "seq", split_axis=2, concat_axis=2, tiled=True)
    arrived = arrived.reshape(
        channels, slot_count * devices, piece_rows, group_count, width // group_count
    )
    picked = [
        chosen(arrived[:, :, :, group_index, :], table[group_index])
        for group_index in range(group_count)
    ]
    fanout = table.shape[1] // devices
    outward = jnp.stack(picked, axis=3).reshape(channels, fanout, devices, piece_rows * width)
    landed = lax.all_to_all(outward, "seq", split_axis=2, concat_axis=2, tiled=True)
    return landed.reshape(channels, fanout, row_count, width)


def route_tables(order, devices):
    device_ids = jnp.arange(devices, dtype=jnp.int32)
    half_ids = jnp.arange(2, dtype=jnp.int32)
    group_count = order.shape[0]
    target = jnp.take(order, device_ids // 2, axis=1)
    both_halves = (2 * target[:, None, :] + half_ids[None, :, None]).reshape(
        group_count, 2 * devices
    )
    same_half = 2 * target + device_ids % 2
    inverse = jnp.argsort(order, axis=1)
    asking = 2 * jnp.take(inverse, device_ids // 2, axis=1)
    returning = (
        (device_ids % 2)[None, None, :] * devices + asking[:, None, :] + half_ids[None, :, None]
    ).reshape(group_count, 2 * devices)
    summed_back = asking + device_ids % 2
    return (both_halves, same_half, returning, summed_back)


def head_view(block_rows):
    return block_rows.reshape(block_rows.shape[0], HEADS, HEAD_DIM)


def group_probs(query_heads, key_heads):
    score_scale = 1.0 / math.sqrt(HEAD_DIM)
    scores = (
        jnp.einsum("qhd,khd->hqk", query_heads, key_heads, preferred_element_type=jnp.float32)
        * score_scale
    )
    top_score = jnp.max(scores, axis=-1, keepdims=True)
    expo_terms = jnp.exp(scores - top_score)
    return expo_terms / jnp.sum(expo_terms, axis=-1, keepdims=True)


def attend_layer(queries, key_rows, value_rows, out_grads):
    score_scale = 1.0 / math.sqrt(HEAD_DIM)
    per_group = HEADS // GROUPS
    query_heads = head_view(queries)
    key_heads = head_view(key_rows)
    value_heads = head_view(value_rows)
    grad_heads = head_view(out_grads)
    attended_out = []
    query_out = []
    key_out = []
    value_out = []
    for group_index in range(GROUPS):
        first_head = group_index * per_group
        last_head = first_head + per_group
        query_group = query_heads[:, first_head:last_head]
        key_group = key_heads[:, first_head:last_head]
        value_group = value_heads[:, first_head:last_head]
        grad_group = grad_heads[:, first_head:last_head]
        probs = group_probs(query_group, key_group)
        probs_low = probs.astype(jnp.bfloat16)
        attended_out.append(
            jnp.einsum(
                "hqk,khd->qhd", probs_low, value_group, preferred_element_type=jnp.float32
            ).astype(jnp.bfloat16)
        )
        grad_probs = jnp.einsum(
            "qhd,khd->hqk", grad_group, value_group, preferred_element_type=jnp.float32
        )
        row_dot = jnp.sum(probs * grad_probs, axis=-1, keepdims=True)
        grad_scores = (probs * (grad_probs - row_dot) * score_scale).astype(jnp.bfloat16)
        query_out.append(
            jnp.einsum(
                "hqk,khd->qhd", grad_scores, key_group, preferred_element_type=jnp.float32
            ).astype(jnp.bfloat16)
        )
        key_out.append(
            jnp.einsum(
                "hqk,qhd->khd", grad_scores, query_group, preferred_element_type=jnp.float32
            ).astype(jnp.bfloat16)
        )
        value_out.append(
            jnp.einsum(
                "hqk,qhd->khd", probs_low, grad_group, preferred_element_type=jnp.float32
            ).astype(jnp.bfloat16)
        )
    key_count = key_rows.shape[0]
    query_count = queries.shape[0]
    return (
        jnp.concatenate(attended_out, axis=1).reshape(query_count, FEATURES),
        jnp.concatenate(query_out, axis=1).reshape(query_count, FEATURES),
        jnp.concatenate(key_out, axis=1).reshape(key_count, FEATURES),
        jnp.concatenate(value_out, axis=1).reshape(key_count, FEATURES),
    )


def head_step(q, g, k_own, k_far, v_own, v_far):
    score_scale = 1.0 / math.sqrt(HEAD_DIM)

    def rows_dot(a, b):
        return lax.dot_general(a, b, (((1,), (1,)), ((), ())), preferred_element_type=jnp.float32)

    def dot(a, b):
        return lax.dot_general(a, b, (((1,), (0,)), ((), ())), preferred_element_type=jnp.float32)

    def cols_dot(a, b):
        return lax.dot_general(a, b, (((0,), (0,)), ((), ())), preferred_element_type=jnp.float32)

    s_own = rows_dot(q, k_own) * score_scale
    s_far = rows_dot(q, k_far) * score_scale
    top = jnp.maximum(
        jnp.max(s_own, axis=-1, keepdims=True), jnp.max(s_far, axis=-1, keepdims=True)
    )
    e_own = jnp.exp(s_own - top)
    e_far = jnp.exp(s_far - top)
    total = jnp.sum(e_own, axis=-1, keepdims=True) + jnp.sum(e_far, axis=-1, keepdims=True)
    inverse = 1.0 / total
    p_own = e_own * inverse
    p_far = e_far * inverse
    b_own = p_own.astype(jnp.bfloat16)
    b_far = p_far.astype(jnp.bfloat16)
    attended = dot(b_own, v_own) + dot(b_far, v_far)
    gp_own = rows_dot(g, v_own)
    gp_far = rows_dot(g, v_far)
    row_dot = jnp.sum(p_own * gp_own, axis=-1, keepdims=True) + jnp.sum(
        p_far * gp_far, axis=-1, keepdims=True
    )
    d_own = (p_own * (gp_own - row_dot) * score_scale).astype(jnp.bfloat16)
    d_far = (p_far * (gp_far - row_dot) * score_scale).astype(jnp.bfloat16)
    grad_query = dot(d_own, k_own) + dot(d_far, k_far)
    return (
        attended,
        grad_query,
        cols_dot(d_own, q),
        cols_dot(b_own, g),
        cols_dot(d_far, q),
        cols_dot(b_far, g),
    )


def fused_kernel(segments, devices, *refs):
    query, key, value, cotangent, block_order = refs[:5]
    passed_out, query_out, key_out, value_out = refs[5:9]
    heads = FEATURES // devices // HEAD_DIM
    full = refs[9 : 9 + heads]
    (back, own_sum, far_sum, order, order_sem, in_s, in_r, passed_s, grad_s, out_r,
     corner_in, next_in) = refs[9 + heads :]
    segment = lax.axis_index("segment")
    seq = lax.axis_index("seq")
    chip = seq // 2
    core = seq % 2
    blocks = devices // 2
    width = FEATURES // devices
    group = seq * width // (FEATURES // GROUPS)
    after = (segment + 1) % segments
    before = (segment + segments - 1) % segments

    def peer(step):
        other = 2 * ((chip // 2 + step // 4) % 2) + (chip + step // 2) % 2
        return 2 * other + (core + step) % 2

    def send(source, target, send_sem, recv_sem, device):
        pltpu.make_async_remote_copy(
            src_ref=source, dst_ref=target, send_sem=send_sem, recv_sem=recv_sem,
            device_id=device, device_id_type=pl.DeviceIdType.MESH,
        ).start()

    def signal(sem, device):
        pl.semaphore_signal(sem, inc=1, device_id=device, device_id_type=pl.DeviceIdType.MESH)

    def take(ref, sem):
        pltpu.make_async_copy(ref, ref, sem).wait()

    barrier = pltpu.get_barrier_semaphore()
    for e in (*NEAR, 1):
        signal(barrier, (segment, peer(e)))

    @pl.when(segment < segments - 1)
    def _():
        signal(barrier, (after, seq))

    def columns(device, head):
        return pl.ds(pl.multiple_of(device * width + head * HEAD_DIM, HEAD_DIM), HEAD_DIM)

    inputs = (query, key, value, cotangent)
    outputs = (passed_out, query_out, key_out, value_out)
    pltpu.make_async_copy(block_order, order, order_sem.at[0]).start()
    pl.semaphore_wait(barrier, len(NEAR) + 1 + jnp.where(segment == 0, 0, 1))

    def spread(head, index, steps):
        for e in steps:
            send(inputs[index].at[0, :, columns(peer(e), head)], full[head].at[index, seq],
                 in_s.at[0], in_r.at[head], (segment, peer(e)))

    signal(corner_in, (segment, peer(2)))
    for index in range(EARLY):
        spread(0, index, NEAR)
    pl.semaphore_wait(corner_in, 1)

    for head in range(heads):
        for index in range(len(inputs)):
            early = head == 0 and index < EARLY
            spread(head, index, [e for e in ORDER if not (early and e in NEAR)])

    @pl.when(segment < segments - 1)
    def _():
        pl.semaphore_wait(next_in, 1)

    signal(next_in, (before, seq))

    @pl.when(segment == segments - 1)
    def _():
        pl.semaphore_wait(next_in, 1)

    for head in range(heads):
        for index, ref in enumerate(inputs):
            pltpu.make_async_copy(
                ref.at[0, :, columns(seq, head)], full[head].at[index, seq], in_r.at[head]
            ).start()
    def compute(head):
        def rows(index, block):
            return full[head][index, pl.ds(2 * block, 2)].reshape(BLOCK, HEAD_DIM)

        def step(block, carry):
            wanted = order[0, group, block]
            att, dq, dk, dv, fk, fv = head_step(
                rows(0, block), rows(3, block), rows(1, block), rows(1, wanted),
                rows(2, block), rows(2, wanted),
            )
            shape = (2, TOK_DEV, HEAD_DIM)
            both = pl.ds(2 * block, 2)
            back[4 * head, both] = att.astype(jnp.bfloat16).reshape(shape)
            back[4 * head + 1, both] = dq.astype(jnp.bfloat16).reshape(shape)
            own_sum[0, block] = dk
            own_sum[1, block] = dv
            far_sum[0, block] = fk
            far_sum[1, block] = fv
            return carry

        lax.fori_loop(0, blocks, step, 0)

        def total(block, carry):
            asking = 0
            for b in range(blocks):
                asking = jnp.where(order[0, group, b] == block, b, asking)
            for which in range(2):
                summed = own_sum[which, block] + far_sum[which, asking]
                back[4 * head + 2 + which, pl.ds(2 * block, 2)] = summed.astype(
                    jnp.bfloat16
                ).reshape(2, TOK_DEV, HEAD_DIM)
            return carry

        lax.fori_loop(0, blocks, total, 0)

    for head in range(heads):
        if head == 0:
            take(order.at[...], order_sem.at[0])
        take(full[head], in_r.at[head])
        compute(head)
        for index, out in enumerate(outputs):
            for e in (*ORDER, 0):
                source = back.at[4 * head + index, peer(e)]
                target = out.at[0, :, columns(seq, head)]
                if index == 0:
                    send(source, target, passed_s.at[0], out_r.at[0], (after, peer(e)))
                elif e:
                    send(source, target, grad_s.at[0], out_r.at[0], (segment, peer(e)))
                else:
                    pltpu.make_async_copy(source, target, out_r.at[0]).start()
    gone = devices - 1
    take(back.at[:, pl.ds(0, gone)], in_s.at[0])
    take(back, out_r.at[0])
    take(back.at[pl.ds(0, heads)], passed_s.at[0])
    take(back.at[pl.ds(0, 3 * heads), pl.ds(0, gone)], grad_s.at[0])


def write_kernel(*refs):
    sems = refs[8]
    copies = [pltpu.make_async_copy(refs[i], refs[4 + i], sems.at[i]) for i in range(4)]
    for copy in copies:
        copy.start()
    for copy in copies:
        copy.wait()


def per_device_fused(query, key, value, cotangent, block_order):
    segments = lax.axis_size("segment")
    devices = lax.axis_size("seq")
    heads = FEATURES // devices // HEAD_DIM
    blocks = devices // 2
    low = jnp.bfloat16
    held = (4, devices, TOK_DEV, HEAD_DIM)
    sums = (2, blocks, BLOCK, HEAD_DIM)
    scratch = [pltpu.VMEM(held, low)] * heads
    scratch += [pltpu.VMEM((4 * heads, *held[1:]), low)]
    scratch += [pltpu.VMEM(sums, jnp.float32)] * 2
    scratch += [pltpu.SMEM(block_order.shape, jnp.int32), pltpu.SemaphoreType.DMA((1,))]
    scratch += [pltpu.SemaphoreType.DMA((1,)), pltpu.SemaphoreType.DMA((heads,))]
    scratch += [pltpu.SemaphoreType.DMA((1,))] * 3 + [pltpu.SemaphoreType.REGULAR] * 2
    whole = pl.BlockSpec(memory_space=pltpu.VMEM)
    out = jax.ShapeDtypeStruct(query.shape, low)
    outs = pl.pallas_call(
        functools.partial(fused_kernel, segments, devices),
        out_shape=(out,) * 4,
        in_specs=[pl.BlockSpec(memory_space=pltpu.HBM)] * 5,
        out_specs=(whole,) * 4,
        scratch_shapes=scratch,
        compiler_params=pltpu.CompilerParams(
            collective_id=0, has_side_effects=True, vmem_limit_bytes=48 * 1024 * 1024
        ),
    )(*[pltpu.with_memory_space_constraint(x, pltpu.HBM) for x in (query, key, value, cotangent, block_order)])
    return pl.pallas_call(
        write_kernel,
        out_shape=(out,) * 4,
        in_specs=[pl.BlockSpec(memory_space=pl.ANY)] * 4,
        out_specs=(pl.BlockSpec(memory_space=pltpu.HBM),) * 4,
        scratch_shapes=[pltpu.SemaphoreType.DMA((4,))],
        compiler_params=pltpu.CompilerParams(vmem_limit_bytes=8 * 1024 * 1024),
    )(*outs)


def per_device_routed(query, key, value, cotangent, block_order):
    devices = lax.axis_size("seq")
    lower_half = lax.axis_index("seq") % 2 == 0
    both_halves, same_half, returning, summed_back = route_tables(block_order[0], devices)
    mine = jnp.stack([key[0], value[0]])
    swapped = partner_rows(mine)
    own_block = jnp.where(
        lower_half,
        jnp.concatenate([mine, swapped], axis=1),
        jnp.concatenate([swapped, mine], axis=1),
    )
    far_block = routed(mine[:, None], both_halves, GROUPS).reshape(2, BLOCK, FEATURES)
    key_sets = jnp.concatenate([own_block, far_block], axis=1)
    attended, grad_queries, key_part, value_part = attend_layer(
        query[0], key_sets[0], key_sets[1], cotangent[0]
    )
    passed_rows = from_behind(attended, "segment", 1)
    partials = jnp.stack([key_part, value_part])
    own_parts = partials[:, :BLOCK]
    far_parts = partials[:, BLOCK:].reshape(2, 2, TOK_DEV, FEATURES)
    kept = jnp.where(lower_half, own_parts[:, :TOK_DEV], own_parts[:, TOK_DEV:])
    given = jnp.where(lower_half, own_parts[:, TOK_DEV:], own_parts[:, :TOK_DEV])
    from_partner = partner_rows(given)
    returned = routed(far_parts, returning, GROUPS)
    matched_low = (returned[:, 0].astype(jnp.float32) + returned[:, 1].astype(jnp.float32)).astype(
        jnp.bfloat16
    )
    matched_terms = lax.optimization_barrier(matched_low).astype(jnp.float32)
    totals = (kept.astype(jnp.float32) + from_partner.astype(jnp.float32) + matched_terms).astype(
        jnp.bfloat16
    )
    return (passed_rows[None], grad_queries[None], totals[0][None], totals[1][None])


def solution(mesh):
    in_specs = (
        P("segment", "seq", None),
        P("segment", "seq", None),
        P("segment", "seq", None),
        P("segment", "seq", None),
        P("segment", None, None),
    )
    out_specs = (
        P("segment", "seq", None),
        P("segment", "seq", None),
        P("segment", "seq", None),
        P("segment", "seq", None),
    )
    fused = mesh.shape["seq"] == 8 and mesh.shape["segment"] > 1
    return jax.shard_map(
        per_device_fused if fused else per_device_routed, mesh=mesh, in_specs=in_specs, out_specs=out_specs, check_vma=False
    )
```

```python
import functools
import math

import jax
import jax.numpy as jnp
from jax import lax
from jax.experimental import pallas as pl
from jax.experimental.pallas import tpu as pltpu
from jax.sharding import PartitionSpec as P

HEADS = 16
HEAD_DIM = 128
GROUPS = 4
BLOCK = 256
TOK_DEV = 128
FEATURES = 2048
ORDER = (4, 2, 6, 5, 3, 7, 1)
NEAR = (2, 4, 3, 5)
EARLY = 1


def from_partner_2(shard, axis, bit):
    return lax.ppermute(shard, axis, [(i, i ^ 1 << bit) for i in range(lax.axis_size(axis))])


def from_behind(value, axis, steps):
    count = lax.axis_size(axis)
    pairs = [(source, (source + steps) % count) for source in range(count)]
    return lax.ppermute(value, axis, pairs)


def partner_rows(stacked):
    return from_partner_2(stacked, "seq", 0)


def chosen(slots, wanted):
    mask = (wanted[:, None] == jnp.arange(slots.shape[1])[None, :]).astype(slots.dtype)
    return jnp.einsum(
        "ts,csrw->ctrw", mask, slots, preferred_element_type=jnp.float32
    ).astype(slots.dtype)


def routed(stacked, table, group_count):
    devices = lax.axis_size("seq")
    channels, slot_count, row_count, width = stacked.shape
    piece_rows = row_count // devices
    pieces = stacked.reshape(channels, slot_count, devices, piece_rows * width)
    arrived = lax.all_to_all(pieces, "seq", split_axis=2, concat_axis=2, tiled=True)
    arrived = arrived.reshape(
        channels, slot_count * devices, piece_rows, group_count, width // group_count
    )
    picked = [
        chosen(arrived[:, :, :, group_index, :], table[group_index])
        for group_index in range(group_count)
    ]
    fanout = table.shape[1] // devices
    outward = jnp.stack(picked, axis=3).reshape(channels, fanout, devices, piece_rows * width)
    landed = lax.all_to_all(outward, "seq", split_axis=2, concat_axis=2, tiled=True)
    return landed.reshape(channels, fanout, row_count, width)


def route_tables(order, devices):
    device_ids = jnp.arange(devices, dtype=jnp.int32)
    half_ids = jnp.arange(2, dtype=jnp.int32)
    group_count = order.shape[0]
    target = jnp.take(order, device_ids // 2, axis=1)
    both_halves = (2 * target[:, None, :] + half_ids[None, :, None]).reshape(
        group_count, 2 * devices
    )
    same_half = 2 * target + device_ids % 2
    inverse = jnp.argsort(order, axis=1)
    asking = 2 * jnp.take(inverse, device_ids // 2, axis=1)
    returning = (
        (device_ids % 2)[None, None, :] * devices + asking[:, None, :] + half_ids[None, :, None]
    ).reshape(group_count, 2 * devices)
    summed_back = asking + device_ids % 2
    return (both_halves, same_half, returning, summed_back)


def head_view(block_rows):
    return block_rows.reshape(block_rows.shape[0], HEADS, HEAD_DIM)


def group_probs(query_heads, key_heads):
    score_scale = 1.0 / math.sqrt(HEAD_DIM)
    scores = (
        jnp.einsum("qhd,khd->hqk", query_heads, key_heads, preferred_element_type=jnp.float32)
        * score_scale
    )
    top_score = jnp.max(scores, axis=-1, keepdims=True)
    expo_terms = jnp.exp(scores - top_score)
    return expo_terms / jnp.sum(expo_terms, axis=-1, keepdims=True)


def attend_layer(queries, key_rows, value_rows, out_grads):
    score_scale = 1.0 / math.sqrt(HEAD_DIM)
    per_group = HEADS // GROUPS
    query_heads = head_view(queries)
    key_heads = head_view(key_rows)
    value_heads = head_view(value_rows)
    grad_heads = head_view(out_grads)
    attended_out = []
    query_out = []
    key_out = []
    value_out = []
    for group_index in range(GROUPS):
        first_head = group_index * per_group
        last_head = first_head + per_group
        query_group = query_heads[:, first_head:last_head]
        key_group = key_heads[:, first_head:last_head]
        value_group = value_heads[:, first_head:last_head]
        grad_group = grad_heads[:, first_head:last_head]
        probs = group_probs(query_group, key_group)
        probs_low = probs.astype(jnp.bfloat16)
        attended_out.append(
            jnp.einsum(
                "hqk,khd->qhd", probs_low, value_group, preferred_element_type=jnp.float32
            ).astype(jnp.bfloat16)
        )
        grad_probs = jnp.einsum(
            "qhd,khd->hqk", grad_group, value_group, preferred_element_type=jnp.float32
        )
        row_dot = jnp.sum(probs * grad_probs, axis=-1, keepdims=True)
        grad_scores = (probs * (grad_probs - row_dot) * score_scale).astype(jnp.bfloat16)
        query_out.append(
            jnp.einsum(
                "hqk,khd->qhd", grad_scores, key_group, preferred_element_type=jnp.float32
            ).astype(jnp.bfloat16)
        )
        key_out.append(
            jnp.einsum(
                "hqk,qhd->khd", grad_scores, query_group, preferred_element_type=jnp.float32
            ).astype(jnp.bfloat16)
        )
        value_out.append(
            jnp.einsum(
                "hqk,qhd->khd", probs_low, grad_group, preferred_element_type=jnp.float32
            ).astype(jnp.bfloat16)
        )
    key_count = key_rows.shape[0]
    query_count = queries.shape[0]
    return (
        jnp.concatenate(attended_out, axis=1).reshape(query_count, FEATURES),
        jnp.concatenate(query_out, axis=1).reshape(query_count, FEATURES),
        jnp.concatenate(key_out, axis=1).reshape(key_count, FEATURES),
        jnp.concatenate(value_out, axis=1).reshape(key_count, FEATURES),
    )


def head_step(q, g, k_own, k_far, v_own, v_far):
    score_scale = 1.0 / math.sqrt(HEAD_DIM)

    def rows_dot(a, b):
        return lax.dot_general(a, b, (((1,), (1,)), ((), ())), preferred_element_type=jnp.float32)

    def dot(a, b):
        return lax.dot_general(a, b, (((1,), (0,)), ((), ())), preferred_element_type=jnp.float32)

    def cols_dot(a, b):
        return lax.dot_general(a, b, (((0,), (0,)), ((), ())), preferred_element_type=jnp.float32)

    s_own = rows_dot(q, k_own) * score_scale
    s_far = rows_dot(q, k_far) * score_scale
    top = jnp.maximum(
        jnp.max(s_own, axis=-1, keepdims=True), jnp.max(s_far, axis=-1, keepdims=True)
    )
    e_own = jnp.exp(s_own - top)
    e_far = jnp.exp(s_far - top)
    total = jnp.sum(e_own, axis=-1, keepdims=True) + jnp.sum(e_far, axis=-1, keepdims=True)
    inverse = 1.0 / total
    p_own = e_own * inverse
    p_far = e_far * inverse
    b_own = p_own.astype(jnp.bfloat16)
    b_far = p_far.astype(jnp.bfloat16)
    attended = dot(b_own, v_own) + dot(b_far, v_far)
    gp_own = rows_dot(g, v_own)
    gp_far = rows_dot(g, v_far)
    row_dot = jnp.sum(p_own * gp_own, axis=-1, keepdims=True) + jnp.sum(
        p_far * gp_far, axis=-1, keepdims=True
    )
    d_own = (p_own * (gp_own - row_dot) * score_scale).astype(jnp.bfloat16)
    d_far = (p_far * (gp_far - row_dot) * score_scale).astype(jnp.bfloat16)
    grad_query = dot(d_own, k_own) + dot(d_far, k_far)
    return (
        attended,
        grad_query,
        cols_dot(d_own, q),
        cols_dot(b_own, g),
        cols_dot(d_far, q),
        cols_dot(b_far, g),
    )


def fused_kernel(segments, devices, *refs):
    query, key, value, cotangent, block_order = refs[:5]
    passed_out, query_out, key_out, value_out = refs[5:9]
    heads = FEATURES // devices // HEAD_DIM
    full = refs[9 : 9 + heads]
    (back, own_sum, far_sum, order, order_sem, in_s, in_r, passed_s, grad_s, out_r,
     corner_in, next_in) = refs[9 + heads :]
    segment = lax.axis_index("segment")
    seq = lax.axis_index("seq")
    chip = seq // 2
    core = seq % 2
    blocks = devices // 2
    width = FEATURES // devices
    group = seq * width // (FEATURES // GROUPS)
    after = (segment + 1) % segments
    before = (segment + segments - 1) % segments

    def peer(step):
        other = 2 * ((chip // 2 + step // 4) % 2) + (chip + step // 2) % 2
        return 2 * other + (core + step) % 2

    def send(source, target, send_sem, recv_sem, device):
        pltpu.make_async_remote_copy(
            src_ref=source, dst_ref=target, send_sem=send_sem, recv_sem=recv_sem,
            device_id=device, device_id_type=pl.DeviceIdType.MESH,
        ).start()

    def signal(sem, device):
        pl.semaphore_signal(sem, inc=1, device_id=device, device_id_type=pl.DeviceIdType.MESH)

    def take(ref, sem):
        pltpu.make_async_copy(ref, ref, sem).wait()

    barrier = pltpu.get_barrier_semaphore()
    for e in (*NEAR, 1):
        signal(barrier, (segment, peer(e)))

    @pl.when(segment < segments - 1)
    def _():
        signal(barrier, (after, seq))

    def columns(device, head):
        return pl.ds(pl.multiple_of(device * width + head * HEAD_DIM, HEAD_DIM), HEAD_DIM)

    inputs = (query, key, value, cotangent)
    outputs = (passed_out, query_out, key_out, value_out)
    pl.semaphore_wait(barrier, len(NEAR) + 1 + jnp.where(segment == 0, 0, 1))

    def spread(head, index, steps):
        for e in steps:
            send(inputs[index].at[0, :, columns(peer(e), head)], full[head].at[index, seq],
                 in_s.at[0], in_r.at[head], (segment, peer(e)))

    signal(corner_in, (segment, peer(2)))
    for index in range(EARLY):
        spread(0, index, NEAR)
    pl.semaphore_wait(corner_in, 1)

    for head in range(heads):
        for index in range(len(inputs)):
            early = head == 0 and index < EARLY
            spread(head, index, [e for e in ORDER if not (early and e in NEAR)])

    @pl.when(segment < segments - 1)
    def _():
        pl.semaphore_wait(next_in, 1)

    signal(next_in, (before, seq))

    @pl.when(segment == segments - 1)
    def _():
        pl.semaphore_wait(next_in, 1)

    pltpu.make_async_copy(block_order, order, order_sem.at[0]).start()
    for head in range(heads):
        for index, ref in enumerate(inputs):
            pltpu.make_async_copy(
                ref.at[0, :, columns(seq, head)], full[head].at[index, seq], in_r.at[head]
            ).start()
    def compute(head):
        def rows(index, block):
            return full[head][index, pl.ds(2 * block, 2)].reshape(BLOCK, HEAD_DIM)

        def step(block, carry):
            wanted = order[0, group, block]
            att, dq, dk, dv, fk, fv = head_step(
                rows(0, block), rows(3, block), rows(1, block), rows(1, wanted),
                rows(2, block), rows(2, wanted),
            )
            shape = (2, TOK_DEV, HEAD_DIM)
            both = pl.ds(2 * block, 2)
            back[4 * head, both] = att.astype(jnp.bfloat16).reshape(shape)
            back[4 * head + 1, both] = dq.astype(jnp.bfloat16).reshape(shape)
            own_sum[0, block] = dk
            own_sum[1, block] = dv
            far_sum[0, block] = fk
            far_sum[1, block] = fv
            return carry

        lax.fori_loop(0, blocks, step, 0)

        def total(block, carry):
            asking = 0
            for b in range(blocks):
                asking = jnp.where(order[0, group, b] == block, b, asking)
            for which in range(2):
                summed = own_sum[which, block] + far_sum[which, asking]
                back[4 * head + 2 + which, pl.ds(2 * block, 2)] = summed.astype(
                    jnp.bfloat16
                ).reshape(2, TOK_DEV, HEAD_DIM)
            return carry

        lax.fori_loop(0, blocks, total, 0)

    for head in range(heads):
        if head == 0:
            take(order.at[...], order_sem.at[0])
        take(full[head], in_r.at[head])
        compute(head)
        for index, out in enumerate(outputs):
            for e in (*ORDER, 0):
                source = back.at[4 * head + index, peer(e)]
                target = out.at[0, :, columns(seq, head)]
                if index == 0:
                    send(source, target, passed_s.at[0], out_r.at[0], (after, peer(e)))
                elif e:
                    send(source, target, grad_s.at[0], out_r.at[0], (segment, peer(e)))
                else:
                    pltpu.make_async_copy(source, target, out_r.at[0]).start()
    gone = devices - 1
    take(back.at[:, pl.ds(0, gone)], in_s.at[0])
    take(back, out_r.at[0])
    take(back.at[pl.ds(0, heads)], passed_s.at[0])
    take(back.at[pl.ds(0, 3 * heads), pl.ds(0, gone)], grad_s.at[0])


def write_kernel(*refs):
    sems = refs[8]
    copies = [pltpu.make_async_copy(refs[i], refs[4 + i], sems.at[i]) for i in range(4)]
    for copy in copies:
        copy.start()
    for copy in copies:
        copy.wait()


def per_device_fused(query, key, value, cotangent, block_order):
    segments = lax.axis_size("segment")
    devices = lax.axis_size("seq")
    heads = FEATURES // devices // HEAD_DIM
    blocks = devices // 2
    low = jnp.bfloat16
    held = (4, devices, TOK_DEV, HEAD_DIM)
    sums = (2, blocks, BLOCK, HEAD_DIM)
    scratch = [pltpu.VMEM(held, low)] * heads
    scratch += [pltpu.VMEM((4 * heads, *held[1:]), low)]
    scratch += [pltpu.VMEM(sums, jnp.float32)] * 2
    scratch += [pltpu.SMEM(block_order.shape, jnp.int32), pltpu.SemaphoreType.DMA((1,))]
    scratch += [pltpu.SemaphoreType.DMA((1,)), pltpu.SemaphoreType.DMA((heads,))]
    scratch += [pltpu.SemaphoreType.DMA((1,))] * 3 + [pltpu.SemaphoreType.REGULAR] * 2
    whole = pl.BlockSpec(memory_space=pltpu.VMEM)
    out = jax.ShapeDtypeStruct(query.shape, low)
    outs = pl.pallas_call(
        functools.partial(fused_kernel, segments, devices),
        out_shape=(out,) * 4,
        in_specs=[pl.BlockSpec(memory_space=pltpu.HBM)] * 5,
        out_specs=(whole,) * 4,
        scratch_shapes=scratch,
        compiler_params=pltpu.CompilerParams(
            collective_id=0, has_side_effects=True, vmem_limit_bytes=48 * 1024 * 1024
        ),
    )(*[pltpu.with_memory_space_constraint(x, pltpu.HBM) for x in (query, key, value, cotangent, block_order)])
    return pl.pallas_call(
        write_kernel,
        out_shape=(out,) * 4,
        in_specs=[pl.BlockSpec(memory_space=pl.ANY)] * 4,
        out_specs=(pl.BlockSpec(memory_space=pltpu.HBM),) * 4,
        scratch_shapes=[pltpu.SemaphoreType.DMA((4,))],
        compiler_params=pltpu.CompilerParams(vmem_limit_bytes=8 * 1024 * 1024),
    )(*outs)


def per_device_routed(query, key, value, cotangent, block_order):
    devices = lax.axis_size("seq")
    lower_half = lax.axis_index("seq") % 2 == 0
    both_halves, same_half, returning, summed_back = route_tables(block_order[0], devices)
    mine = jnp.stack([key[0], value[0]])
    swapped = partner_rows(mine)
    own_block = jnp.where(
        lower_half,
        jnp.concatenate([mine, swapped], axis=1),
        jnp.concatenate([swapped, mine], axis=1),
    )
    far_block = routed(mine[:, None], both_halves, GROUPS).reshape(2, BLOCK, FEATURES)
    key_sets = jnp.concatenate([own_block, far_block], axis=1)
    attended, grad_queries, key_part, value_part = attend_layer(
        query[0], key_sets[0], key_sets[1], cotangent[0]
    )
    passed_rows = from_behind(attended, "segment", 1)
    partials = jnp.stack([key_part, value_part])
    own_parts = partials[:, :BLOCK]
    far_parts = partials[:, BLOCK:].reshape(2, 2, TOK_DEV, FEATURES)
    kept = jnp.where(lower_half, own_parts[:, :TOK_DEV], own_parts[:, TOK_DEV:])
    given = jnp.where(lower_half, own_parts[:, TOK_DEV:], own_parts[:, :TOK_DEV])
    from_partner = partner_rows(given)
    returned = routed(far_parts, returning, GROUPS)
    matched_low = (returned[:, 0].astype(jnp.float32) + returned[:, 1].astype(jnp.float32)).astype(
        jnp.bfloat16
    )
    matched_terms = lax.optimization_barrier(matched_low).astype(jnp.float32)
    totals = (kept.astype(jnp.float32) + from_partner.astype(jnp.float32) + matched_terms).astype(
        jnp.bfloat16
    )
    return (passed_rows[None], grad_queries[None], totals[0][None], totals[1][None])


def solution(mesh):
    in_specs = (
        P("segment", "seq", None),
        P("segment", "seq", None),
        P("segment", "seq", None),
        P("segment", "seq", None),
        P("segment", None, None),
    )
    out_specs = (
        P("segment", "seq", None),
        P("segment", "seq", None),
        P("segment", "seq", None),
        P("segment", "seq", None),
    )
    fused = mesh.shape["seq"] == 8 and mesh.shape["segment"] > 1
    return jax.shard_map(
        per_device_fused if fused else per_device_routed, mesh=mesh, in_specs=in_specs, out_specs=out_specs, check_vma=False
    )
```
